32 devices in a mesh: lat: 8 (over z, core), lon: 4 (over y, x).
Axes of the slice: x: 2, y: 2, z: 4, core: 2. Of those that a mesh axis runs over, the one named last changes fastest.
Arguments:
- ensemble: float32 [80, 1, 256, 512], P(None, None, 'lat', 'lon'), may hold values from -6 to 6
- obs_value: float32 [4, 8, 4, 128], P(None, 'lat', 'lon'), may hold values from -6 to 6
- obs_error: float32 [4, 8, 4, 128], P(None, 'lat', 'lon'), may hold values from 0.25 to 4
- obs_cell: int32 [4, 8, 4, 128], P(None, 'lat', 'lon'), may hold values from 0 to 4095
- obs_radius: int32 [4, 8, 4, 128], P(None, 'lat', 'lon'), may hold values from 8 to 32
- obs_count: int32 [4, 8, 4], P(None, 'lat', 'lon'), may hold values from 16 to 128, as said below
- batch_order: int32 [4], replicated, may hold values from 0 to 3, each once
Outputs:
- analysis: float32 [80, 1, 256, 512], P(None, None, 'lat', 'lon')
The draws below stay inside these ranges and needn't reach their ends.
Inputs may be any that keep to these rules, and one draw needn't show every extreme that they name: `obs_count`: slots at or beyond the count hold no observation and are ignored. In every batch some tile has all 128 slots live.
All inputs are finite; a program needn't handle non-finite values.
Results may differ from the reference program's by a relative error of at most 0.0021.
Values may be sent and summed in bfloat16 or wider, within the bound.
A program may use at most 64 MiB of HBM per device.

```python
import math
import jax
import jax.numpy as jnp
from jax import lax

M = 80
LEV = 1
CLAT = 32
CLON = 128
CAP = 128
NB = 4
RMAX = 32
NLAT = 256
NLON = 512
N_LAT = 8
N_LON = 4


def draw_obs_count(key, part):
    first_key, second_key = jax.random.split(jax.random.fold_in(key, 17))
    halvings = jax.random.randint(first_key, (NB, N_LAT, N_LON), 0, 4)
    full_tile = jax.random.randint(second_key, (NB, 1, 1), 0, N_LAT * N_LON)
    tile_ids = jnp.arange(N_LAT, dtype=jnp.int32)[:, None] * N_LON + jnp.arange(N_LON, dtype=jnp.int32)[None, :]
    halvings = jnp.where(tile_ids[None] == full_tile, 0, halvings)
    return jnp.right_shift(jnp.full((NB, N_LAT, N_LON), CAP, jnp.int32), halvings.astype(jnp.int32)).astype(jnp.int32)


def place_ends(array, stream_key, least, top_value):
    dims = array.shape
    index_at = [jax.random.randint(jax.random.fold_in(stream_key, axis), (), 0, dims[axis]) for axis in range(len(dims))]
    array = array.at[tuple(index_at)].set(least)
    longest = dims.index(max(dims))
    index_at[longest] = (index_at[longest] + 1) % dims[longest]
    return array.at[tuple(index_at)].set(top_value)


def block_scale(own_key, extent, shards, smallest, largest):
    level = 1.0
    for position, parts in shards:
        heights = jax.random.uniform(jax.random.fold_in(jax.random.fold_in(own_key, 6), position), (parts,), jnp.float32, smallest / len(shards), largest / len(shards))
        level = level * jnp.repeat(jnp.exp(heights), extent[position] // parts).reshape((-1,) + (1,) * (len(extent) - 1 - position))
    return level


def scatter_about(own_key, shape, deviation, most, shards=(), kind=jnp.bfloat16):
    array = deviation * jax.random.normal(own_key, shape, jnp.float32)
    if shards:
        array = array * block_scale(own_key, shape, shards, -0.22, 0.18)
    return jnp.clip(array, -most, most).astype(kind)


def setup_inputs(seed: int = 0) -> dict:
    streams_of = jax.random.split(jax.random.key(seed), 8)
    return {
        "ensemble": scatter_about(streams_of[0], (M, LEV, NLAT, NLON), 1.0, 6.0, ((2, 8), (3, 4)), jnp.float32),
        "obs_value": scatter_about(streams_of[1], (NB, N_LAT, N_LON, CAP), 1.0, 6.0, ((1, 8), (2, 4)), jnp.float32),
        "obs_error": jnp.clip(jnp.exp(math.log(4.0) - 2.7725887 * jax.random.uniform(streams_of[2], (NB, N_LAT, N_LON, CAP), jnp.float32) ** block_scale(streams_of[2], (NB, N_LAT, N_LON, CAP), ((1, 8), (2, 4)), -0.2, 0.2)), 0.25, 4.0),
        "obs_cell": place_ends(jax.random.randint(streams_of[3], (NB, N_LAT, N_LON, CAP), 0, CLAT * CLON), jax.random.fold_in(streams_of[3], 1), 0, (CLAT * CLON) - 1).astype(jnp.int32),
        "obs_radius": place_ends(jax.random.randint(streams_of[4], (NB, N_LAT, N_LON, CAP), RMAX // 4, RMAX + 1), jax.random.fold_in(streams_of[4], 1), RMAX // 4, RMAX).astype(jnp.int32),
        "obs_count": draw_obs_count(jax.random.fold_in(streams_of[7], 71), 0),
        "batch_order": jax.random.permutation(streams_of[6], NB).astype(jnp.int32),
    }


def observe_stats(priors, values, errors, is_live):
    members = priors.shape[0]
    prior_mean = lax.optimization_barrier(jnp.mean(priors, axis=0))
    spread = priors - prior_mean
    variance = lax.optimization_barrier(jnp.sum(spread * spread, axis=0)) / (members - 1)
    denom_total = variance + errors
    shrink = 1.0 / (1.0 + jnp.sqrt(errors / denom_total))
    factor = 1.0 / ((members - 1) * denom_total)
    obs_pert = jnp.where(is_live, spread, 0.0).astype(jnp.bfloat16)
    obs_gain = jnp.where(is_live, factor * (values - prior_mean - shrink * spread), 0.0).astype(jnp.bfloat16)
    return (obs_pert, obs_gain)

def assimilate(current, obs_pert, obs_gain, where_ints, lat_base, lon_base, full_lon, block_cols):
    members, levels, lat_rows, lon_cols = current.shape
    cells = lat_rows * lon_cols
    flat_state = current.reshape(members, levels, cells)
    centered = (flat_state - lax.optimization_barrier(jnp.mean(flat_state, axis=0))).astype(jnp.bfloat16)
    obs_lat = where_ints[0]
    obs_lon = where_ints[1]
    cutoff = where_ints[2]
    cutoff_sq = cutoff * cutoff
    width_sq = jnp.maximum(cutoff_sq, 1).astype(jnp.float32)

    def one_block(block_id, total_inc):
        first_col = block_id * block_cols
        positions = first_col + jnp.arange(block_cols, dtype=jnp.int32)
        cell_lat = lat_base + positions // lon_cols
        cell_lon = lon_base + positions % lon_cols
        lat_gap = cell_lat[:, None] - obs_lat[None, :]
        lon_gap = jnp.abs(cell_lon[:, None] - obs_lon[None, :])
        lon_dist = jnp.minimum(lon_gap, full_lon - lon_gap)
        dist_sq = lat_gap * lat_gap + lon_dist * lon_dist
        weights = jnp.where(dist_sq <= cutoff_sq[None, :], jnp.exp(-2.0 * dist_sq.astype(jnp.float32) / width_sq[None, :]), 0.0)
        centered_block = lax.dynamic_slice_in_dim(centered, first_col, block_cols, 2).reshape(members, levels * block_cols)
        covariance = lax.dot_general(centered_block, obs_pert, (((0,), (0,)), ((), ())), preferred_element_type=jnp.float32)
        scaled = (covariance.reshape(levels, block_cols, -1) * weights[None]).astype(jnp.bfloat16).reshape(levels * block_cols, -1)
        increment = lax.dot_general(obs_gain, scaled, (((1,), (1,)), ((), ())), preferred_element_type=jnp.float32)
        return lax.dynamic_update_slice_in_dim(total_inc, increment.reshape(members, levels, block_cols), first_col, 2)
    total_inc = lax.fori_loop(0, cells // block_cols, one_block, jnp.zeros_like(flat_state))
    return (flat_state + total_inc).reshape(current.shape)

def neighbors(packed):
    padded = jnp.pad(packed, ((0, 0), (1, 1), (0, 0), (0, 0)))
    pieces = []
    for lat_move in (1, 0, -1):
        lat_band = padded[:, 1 - lat_move:1 - lat_move + N_LAT]
        for lon_move in (1, 0, -1):
            pieces.append(jnp.roll(lat_band, lon_move, axis=2))
    return jnp.concatenate(pieces, axis=3)

def reference(ensemble, obs_value, obs_error, obs_cell, obs_radius, obs_count, batch_order):
    tile_total = N_LAT * N_LON
    tile_ids = jnp.arange(tile_total, dtype=jnp.int32)
    tile_lat = tile_ids // N_LON * CLAT
    tile_lon = tile_ids % N_LON * CLON
    lat_start = (jnp.arange(N_LAT, dtype=jnp.int32) * CLAT)[:, None, None]
    lon_start = (jnp.arange(N_LON, dtype=jnp.int32) * CLON)[None, :, None]
    slot_ids = jnp.arange(CAP, dtype=jnp.int32)[None, None, :]
    current = ensemble
    for batch_step in range(NB):
        chosen = batch_order[batch_step]
        cell_ids = obs_cell[chosen]
        obs_lat = (lat_start + cell_ids // CLON).astype(jnp.int32)
        obs_lon = (lon_start + cell_ids % CLON).astype(jnp.int32)
        priors = current[:, 0][:, obs_lat, obs_lon]
        is_live = slot_ids < obs_count[chosen][:, :, None]
        obs_pert, obs_gain = observe_stats(priors, obs_value[chosen], obs_error[chosen], is_live)
        where_ints = jnp.stack([obs_lat, obs_lon, obs_radius[chosen]]).astype(jnp.int32)
        pert_near = neighbors(obs_pert).transpose(1, 2, 0, 3).reshape(tile_total, M, 9 * CAP)
        gain_near = neighbors(obs_gain).transpose(1, 2, 0, 3).reshape(tile_total, M, 9 * CAP)
        ints_near = neighbors(where_ints).transpose(1, 2, 0, 3).reshape(tile_total, 3, 9 * CAP)
        tile_blocks = current.reshape(M, LEV, N_LAT, CLAT, N_LON, CLON).transpose(2, 4, 0, 1, 3, 5).reshape(tile_total, M, LEV, CLAT, CLON)

        def tile_step(operands):
            one_tile, pert_tile, gain_tile, ints_tile, lat_base, lon_base = operands
            return assimilate(one_tile, pert_tile, gain_tile, ints_tile, lat_base, lon_base, NLON, CLAT * CLON)
        updated = lax.map(tile_step, (tile_blocks, pert_near, gain_near, ints_near, tile_lat, tile_lon))
        current = updated.reshape(N_LAT, N_LON, M, LEV, CLAT, CLON).transpose(2, 3, 0, 4, 1, 5).reshape(M, LEV, NLAT, NLON)
    return current
```

```python
import functools

import jax
import jax.numpy as jnp
from jax import lax
from jax.experimental import pallas as pl
from jax.experimental.pallas import tpu as pltpu
from jax.sharding import PartitionSpec as P

REACH = 32
LANES = 128
GROUP = 8

OFFSETS = ((0, 0), (-1, 0), (1, 0), (-1, -1), (0, -1), (1, -1), (-1, 1), (0, 1), (1, 1))
NORTH = tuple(t for t, (dy, _) in enumerate(OFFSETS) if dy < 0)
SOUTH = tuple(t for t, (dy, _) in enumerate(OFFSETS) if dy > 0)
LEVEL = tuple(t for t, (dy, dx) in enumerate(OFFSETS) if dy == 0 and dx != 0)


def opposite(slot):
    dy, dx = OFFSETS[slot]
    return OFFSETS.index((-dy, -dx))


def split3(value):
    high = value.astype(jnp.bfloat16)
    rest = value - high.astype(jnp.float32)
    mid = rest.astype(jnp.bfloat16)
    low = rest - mid.astype(jnp.float32)
    return high.astype(jnp.float32), mid.astype(jnp.float32), low


def kernel(
    dims,
    order_s,
    count_s,
    cell_s,
    x_ref,
    value_ref,
    error_ref,
    cell_ref,
    radius_ref,
    out_ref,
    xt,
    cent,
    hx,
    packets,
    hp_all,
    gain_all,
    reach_lat,
    decay_lat,
    gap_mid,
    decay_mid,
    gap_side,
    decay_side,
    send_sem,
    recv_sem,
):
    members, rows, cols, slots, batches, n_lat, n_lon = dims
    padded = xt.shape[1]
    chunks = cols // REACH
    chunk_cells = rows * REACH
    row_groups = rows // GROUP
    block = GROUP * REACH
    f32, bf16 = jnp.float32, jnp.bfloat16
    lat = lax.axis_index("lat")
    lon = lax.axis_index("lon")
    has_north = lat > 0
    has_south = lat < n_lat - 1

    def device(slot):
        dy, dx = OFFSETS[slot]
        return (lat + dy, lax.rem(lon + dx + n_lon, n_lon))

    def at_sides(action):
        for slot in LEVEL:
            action(slot)

        @pl.when(has_north)
        def _():
            for slot in NORTH:
                action(slot)

        @pl.when(has_south)
        def _():
            for slot in SOUTH:
                action(slot)

    packets[...] = jnp.zeros_like(packets)
    barrier = pltpu.get_barrier_semaphore()

    def greet(slot):
        pl.semaphore_signal(
            barrier, inc=1, device_id=device(slot), device_id_type=pl.DeviceIdType.MESH
        )

    at_sides(greet)

    hp_all[...] = jnp.zeros_like(hp_all)
    gain_all[...] = jnp.zeros_like(gain_all)

    def centre(start, size):
        x = xt[pl.ds(start, size), :]
        mean = jnp.sum(x, axis=1, keepdims=True) * (1.0 / members)
        cent[pl.ds(start, size), :] = (x - mean).astype(bf16)

    def load_row(r, carry):
        v = x_ref[pl.ds(r, members, stride=rows), :]
        v = jnp.concatenate([v, jnp.zeros((padded - members, cols), f32)], axis=0)
        vt = jnp.transpose(v)
        mean = jnp.sum(vt, axis=1, keepdims=True) * (1.0 / members)
        vc = (vt - mean).astype(bf16)
        for q in range(chunks):
            start = pl.multiple_of(q * chunk_cells + r * REACH, REACH)
            xt[pl.ds(start, REACH), :] = vt[q * REACH : (q + 1) * REACH]
            cent[pl.ds(start, REACH), :] = vc[q * REACH : (q + 1) * REACH]
        return carry

    lax.fori_loop(0, rows, load_row, 0)

    above = (lat + n_lat - 1) // n_lat
    below = (2 * n_lat - 2 - lat) // n_lat
    pl.semaphore_wait(barrier, len(LEVEL) + len(NORTH) * above + len(SOUTH) * below)

    def outgoing(k, slot):
        there = opposite(slot)
        return pltpu.make_async_remote_copy(
            src_ref=packets.at[k, 0],
            dst_ref=packets.at[k, there],
            send_sem=send_sem.at[k, slot],
            recv_sem=recv_sem.at[k, there],
            device_id=device(slot),
            device_id_type=pl.DeviceIdType.MESH,
        )

    def incoming(k, slot):
        return pltpu.make_async_remote_copy(
            src_ref=packets.at[k, 0],
            dst_ref=packets.at[k, slot],
            send_sem=send_sem.at[k, slot],
            recv_sem=recv_sem.at[k, slot],
            device_id=device(slot),
            device_id_type=pl.DeviceIdType.MESH,
        )

    def unpack(k, slot):
        dy, dx = OFFSETS[slot]
        lanes = slice(slot * slots, (slot + 1) * slots)
        packet = packets[k, slot]
        hp = packet[:members]
        tail = packet[members:].astype(f32)
        base = tail[0:1] + tail[1:2] + tail[2:3]
        slope = tail[3:4] + tail[4:5] + tail[5:6]
        radius = tail[8:9]
        hp_all[:members, lanes] = hp
        gain_all[:members, lanes] = (base - slope * hp.astype(f32)).astype(bf16)
        reach2 = radius * radius
        rate = -2.0 / jnp.maximum(reach2, 1.0)
        row_ids = lax.broadcasted_iota(jnp.int32, (rows, slots), 0).astype(f32)
        dlat = row_ids - (tail[6:7] + float(dy * rows))
        dlat2 = dlat * dlat
        reach_lat[:, lanes] = reach2 - dlat2
        decay_lat[:, lanes] = jnp.exp(dlat2 * rate)
        if dx == 0:
            col_ids = lax.broadcasted_iota(jnp.int32, (cols, slots), 0).astype(f32)
            dlon = col_ids - tail[7:8]
            gap_ref, decay_ref, here = gap_mid, decay_mid, lanes
        else:
            first = 0 if dx < 0 else cols - REACH
            col_ids = lax.broadcasted_iota(jnp.int32, (REACH, slots), 0).astype(f32)
            dlon = col_ids + float(first - dx * cols) - tail[7:8]
            gap_ref, decay_ref = gap_side, decay_side
            here = slice((slot - 3) * slots, (slot - 2) * slots)
        dlon2 = dlon * dlon
        gap_ref[:, here] = dlon2
        decay_ref[:, here] = jnp.exp(dlon2 * rate)

    def update(q, group, first_slot, n_slots, side, centring):
        lanes = slice(first_slot * slots, (first_slot + n_slots) * slots)
        width = n_slots * slots
        cells = pl.ds(pl.multiple_of(q * chunk_cells + group * block, block), block)
        cov = jnp.dot(cent[cells, :], hp_all[:, lanes], preferred_element_type=f32)
        if side:
            here = slice((first_slot - 3) * slots, (first_slot - 3 + n_slots) * slots)
            gap, decay = gap_side[:, here], decay_side[:, here]
        else:
            columns = pl.ds(pl.multiple_of(q * REACH, REACH), REACH)
            gap, decay = gap_mid[columns, lanes], decay_mid[columns, lanes]
        lat_rows = pl.ds(pl.multiple_of(group * GROUP, GROUP), GROUP)
        reach = reach_lat[lat_rows, lanes]
        fade = decay_lat[lat_rows, lanes]
        parts = []
        for r in range(GROUP):
            weight = jnp.where(gap <= reach[r : r + 1], decay * fade[r : r + 1], 0.0)
            parts.append((cov[r * REACH : (r + 1) * REACH] * weight).astype(bf16))
        scaled = jnp.concatenate(parts, axis=0)
        inc = lax.dot_general(
            scaled, gain_all[:, lanes], (((1,), (1,)), ((), ())), preferred_element_type=f32
        )
        x = xt[cells, :] + inc
        xt[cells, :] = x
        if centring:
            mean = jnp.sum(x, axis=1, keepdims=True) * (1.0 / members)
            cent[cells, :] = (x - mean).astype(bf16)

    def sweep(first_q, n_q, first_slot, n_slots, side=False, centring=False):
        def step(i, carry):
            q = first_q + i // row_groups
            update(q, i % row_groups, first_slot, n_slots, side, centring)
            return carry

        lax.fori_loop(0, n_q * row_groups, step, 0)

    def one_batch(k, carry):
        chosen = order_s[k]

        def gather(i, inner):
            for j in range(8):
                s = i * 8 + j
                cell = cell_s[chosen, 0, 0, s]
                row = cell // cols
                col = cell % cols
                place = (col // REACH) * chunk_cells + row * REACH + col % REACH
                hx[pl.ds(s, 1), :] = xt[pl.ds(place, 1), :]
            return inner

        lax.fori_loop(0, slots // 8, gather, 0)
        prior = jnp.transpose(hx[...])[:members]
        mean = jnp.sum(prior, axis=0, keepdims=True) * (1.0 / members)
        pert = prior - mean
        var = jnp.sum(pert * pert, axis=0, keepdims=True) * (1.0 / (members - 1))
        error = error_ref[chosen, 0]
        total = var + error
        shrink = 1.0 / (1.0 + jnp.sqrt(error / total))
        factor = 1.0 / ((members - 1) * total)
        live = lax.broadcasted_iota(jnp.int32, (1, slots), 1) < count_s[chosen, 0, 0]
        base = jnp.where(live, factor * (value_ref[chosen, 0] - mean), 0.0)
        slope = jnp.where(live, factor * shrink, 0.0)
        cell = cell_ref[chosen, 0]
        tail = jnp.concatenate(
            [
                *split3(base),
                *split3(slope),
                (cell // cols).astype(f32),
                (cell % cols).astype(f32),
                radius_ref[chosen, 0].astype(f32),
                jnp.zeros((7, slots), f32),
            ],
            axis=0,
        )
        packets[k, 0, :members, :] = jnp.where(live, pert, 0.0).astype(bf16)
        packets[k, 0, members:, :] = tail.astype(bf16)
        at_sides(lambda slot: outgoing(k, slot).start())

        unpack(k, 0)
        sweep(0, chunks, 0, 1)

        @pl.when(has_north)
        def _():
            incoming(k, 1).wait_recv()

        @pl.when(has_south)
        def _():
            incoming(k, 2).wait_recv()

        unpack(k, 1)
        unpack(k, 2)
        sweep(1, chunks - 2, 1, 2, centring=True)
        sweep(0, 1, 1, 2)
        sweep(chunks - 1, 1, 1, 2)

        for slot in LEVEL:
            incoming(k, slot).wait_recv()

        @pl.when(has_north)
        def _():
            for slot in NORTH[1:]:
                incoming(k, slot).wait_recv()

        @pl.when(has_south)
        def _():
            for slot in SOUTH[1:]:
                incoming(k, slot).wait_recv()

        for slot in range(3, 9):
            unpack(k, slot)
        sweep(0, 1, 3, 3, side=True, centring=True)
        sweep(chunks - 1, 1, 6, 3, side=True, centring=True)
        at_sides(lambda slot: outgoing(k, slot).wait_send())
        return carry

    lax.fori_loop(0, batches, one_batch, 0)

    def store_row(r, carry):
        pieces = [
            xt[pl.ds(pl.multiple_of(q * chunk_cells + r * REACH, REACH), REACH), :]
            for q in range(chunks)
        ]
        v = jnp.transpose(jnp.concatenate(pieces, axis=0))
        out_ref[pl.ds(r, members, stride=rows), :] = v[:members]
        return carry

    lax.fori_loop(0, rows, store_row, 0)


def local(ensemble, obs_value, obs_error, obs_cell, obs_radius, obs_count, batch_order):
    members, levels, rows, cols = ensemble.shape
    batches = obs_cell.shape[0]
    slots = obs_cell.shape[-1]
    assert levels == 1 and cols == LANES and slots == LANES and rows == REACH
    n_lat, n_lon = lax.axis_size("lat"), lax.axis_size("lon")
    padded = -(-members // LANES) * LANES
    cells = rows * cols
    tiles = len(OFFSETS)
    vmem = pl.BlockSpec(memory_space=pltpu.VMEM)
    smem = pl.BlockSpec(memory_space=pltpu.SMEM)
    f32, bf16 = jnp.float32, jnp.bfloat16
    out = pl.pallas_call(
        functools.partial(kernel, (members, rows, cols, slots, batches, n_lat, n_lon)),
        out_shape=jax.ShapeDtypeStruct((members * rows, cols), f32),
        in_specs=[smem, smem, smem, vmem, vmem, vmem, vmem, vmem],
        out_specs=vmem,
        scratch_shapes=[
            pltpu.VMEM((cells, padded), f32),
            pltpu.VMEM((cells, padded), bf16),
            pltpu.VMEM((slots, padded), f32),
            pltpu.VMEM((batches, tiles, members + 16, slots), bf16),
            pltpu.VMEM((padded, tiles * slots), bf16),
            pltpu.VMEM((padded, tiles * slots), bf16),
            pltpu.VMEM((rows, tiles * slots), f32),
            pltpu.VMEM((rows, tiles * slots), f32),
            pltpu.VMEM((cols, 3 * slots), f32),
            pltpu.VMEM((cols, 3 * slots), f32),
            pltpu.VMEM((REACH, 6 * slots), f32),
            pltpu.VMEM((REACH, 6 * slots), f32),
            pltpu.SemaphoreType.DMA((batches, tiles)),
            pltpu.SemaphoreType.DMA((batches, tiles)),
        ],
        compiler_params=pltpu.CompilerParams(
            collective_id=0, has_side_effects=True, vmem_limit_bytes=32 * 1024 * 1024
        ),
    )(
        batch_order,
        obs_count,
        obs_cell,
        ensemble.reshape(members * rows, cols),
        obs_value,
        obs_error,
        obs_cell,
        obs_radius,
    )
    return out.reshape(ensemble.shape)


def solution(mesh):
    return jax.shard_map(
        local,
        mesh=mesh,
        in_specs=(
            P(None, None, "lat", "lon"),
            P(None, "lat", "lon", None),
            P(None, "lat", "lon", None),
            P(None, "lat", "lon", None),
            P(None, "lat", "lon", None),
            P(None, "lat", "lon"),
            P(),
        ),
        out_specs=P(None, None, "lat", "lon"),
        check_vma=False,
    )
```

```python
import functools

import jax
import jax.numpy as jnp
from jax import lax
from jax.experimental import pallas as pl
from jax.experimental.pallas import tpu as pltpu
from jax.sharding import PartitionSpec as P

REACH = 32
LANES = 128
COL_BITS = 7
REACH_BITS = 5
TAIL = 16
UNROLL = 8
GROUP = 8

OFFSETS = ((0, 0), (-1, 0), (1, 0), (-1, -1), (0, -1), (1, -1), (-1, 1), (0, 1), (1, 1))
NORTH, SOUTH, WEST, EAST = 1, 2, 4, 7


def repeat(count, unroll, body):
    def step(i, carry):
        for j in range(unroll):
            body(i * unroll + j)
        return carry

    lax.fori_loop(0, count // unroll, step, 0)


def opposite(slot):
    dy, dx = OFFSETS[slot]
    return OFFSETS.index((-dy, -dx))


def kernel(
    dims,
    order_s,
    count_s,
    cell_s,
    x_ref,
    value_ref,
    error_ref,
    cell_ref,
    radius_ref,
    out_ref,
    xt,
    cent,
    hx,
    packets,
    hp_all,
    gain_all,
    reach_lat,
    decay_lat,
    gap_mid,
    decay_mid,
    gap_side,
    decay_side,
    send_sem,
    recv_sem,
):
    members, rows, cols, slots, batches, n_lat, n_lon = dims
    padded = xt.shape[1]
    chunks = cols // REACH
    chunk_cells = rows * REACH
    row_groups = rows // GROUP
    block = GROUP * REACH
    f32, bf16 = jnp.float32, jnp.bfloat16
    lat = lax.axis_index("lat")
    lon = lax.axis_index("lon")
    has_north = lat > 0
    has_south = lat < n_lat - 1

    def device(slot):
        dy, dx = OFFSETS[slot]
        return (lat + dy, lax.rem(lon + dx + n_lon, n_lon))

    def at_sides(action):
        for slot in (WEST, EAST):
            action(slot)

        @pl.when(has_north)
        def _():
            for slot in (1, 3, 6):
                action(slot)

        @pl.when(has_south)
        def _():
            for slot in (2, 5, 8):
                action(slot)

    packets[...] = jnp.zeros_like(packets)
    barrier = pltpu.get_barrier_semaphore()

    def greet(slot):
        pl.semaphore_signal(
            barrier, inc=1, device_id=device(slot), device_id_type=pl.DeviceIdType.MESH
        )

    at_sides(greet)

    hp_all[...] = jnp.zeros_like(hp_all)
    gain_all[...] = jnp.zeros_like(gain_all)

    def centre(start, size):
        x = xt[pl.ds(start, size), :]
        mean = jnp.sum(x, axis=1, keepdims=True) * (1.0 / members)
        cent[pl.ds(start, size), :] = (x - mean).astype(bf16)

    def load_row(r):
        v = x_ref[pl.ds(r, members, stride=rows), :]
        v = jnp.concatenate([v, jnp.zeros((padded - members, cols), f32)], axis=0)
        vt = jnp.transpose(v)
        mean = jnp.sum(vt, axis=1, keepdims=True) * (1.0 / members)
        vc = (vt - mean).astype(bf16)
        for q in range(chunks):
            start = pl.multiple_of(q * chunk_cells + r * REACH, REACH)
            xt[pl.ds(start, REACH), :] = vt[q * REACH : (q + 1) * REACH]
            cent[pl.ds(start, REACH), :] = vc[q * REACH : (q + 1) * REACH]

    repeat(rows, 4, load_row)

    above = (lat + n_lat - 1) // n_lat
    below = (2 * n_lat - 2 - lat) // n_lat
    pl.semaphore_wait(barrier, 2 + 3 * above + 3 * below)

    def moved(k, source, target, sender, toward):
        return pltpu.make_async_remote_copy(
            src_ref=packets.at[k, source],
            dst_ref=packets.at[k, target],
            send_sem=send_sem.at[k, sender],
            recv_sem=recv_sem.at[k, target],
            device_id=device(toward),
            device_id_type=pl.DeviceIdType.MESH,
        )

    def outgoing(k, slot):
        return moved(k, 0, opposite(slot), slot, slot)

    def incoming(k, slot):
        return moved(k, 0, slot, slot, EAST)

    def unpack(k, slot):
        dy, dx = OFFSETS[slot]
        lanes = slice(slot * slots, (slot + 1) * slots)
        packet = packets[k, slot]
        hp = packet[:members]
        tail = packet[2 * members :].astype(f32)
        radius = tail[2:3]
        hp_all[:members, lanes] = hp
        gain_all[:members, lanes] = packet[members : 2 * members]
        reach2 = radius * radius
        rate = -2.0 / jnp.maximum(reach2, 1.0)
        row_ids = lax.broadcasted_iota(jnp.int32, (rows, slots), 0).astype(f32)
        dlat = row_ids - (tail[0:1] + float(dy * rows))
        dlat2 = dlat * dlat
        reach_lat[:, lanes] = reach2 - dlat2
        decay_lat[:, lanes] = jnp.exp(dlat2 * rate)
        if dx == 0:
            col_ids = lax.broadcasted_iota(jnp.int32, (cols, slots), 0).astype(f32)
            dlon = col_ids - tail[1:2]
            gap_ref, decay_ref, here = gap_mid, decay_mid, lanes
        else:
            first = 0 if dx < 0 else cols - REACH
            col_ids = lax.broadcasted_iota(jnp.int32, (REACH, slots), 0).astype(f32)
            dlon = col_ids + float(first - dx * cols) - tail[1:2]
            gap_ref, decay_ref = gap_side, decay_side
            here = slice((slot - 3) * slots, (slot - 2) * slots)
        dlon2 = dlon * dlon
        gap_ref[:, here] = dlon2
        decay_ref[:, here] = jnp.exp(dlon2 * rate)

    def update(q, group, first_slot, n_slots, side, centring):
        lanes = slice(first_slot * slots, (first_slot + n_slots) * slots)
        width = n_slots * slots
        cells = pl.ds(pl.multiple_of(q * chunk_cells + group * block, block), block)
        cov = jnp.dot(cent[cells, :], hp_all[:, lanes], preferred_element_type=f32)
        if side:
            here = slice((first_slot - 3) * slots, (first_slot - 3 + n_slots) * slots)
            gap, decay = gap_side[:, here], decay_side[:, here]
        else:
            columns = pl.ds(pl.multiple_of(q * REACH, REACH), REACH)
            gap, decay = gap_mid[columns, lanes], decay_mid[columns, lanes]
        lat_rows = pl.ds(pl.multiple_of(group * GROUP, GROUP), GROUP)
        reach = reach_lat[lat_rows, lanes]
        fade = decay_lat[lat_rows, lanes]
        parts = []
        for r in range(GROUP):
            weight = jnp.where(gap <= reach[r : r + 1], decay * fade[r : r + 1], 0.0)
            parts.append((cov[r * REACH : (r + 1) * REACH] * weight).astype(bf16))
        scaled = jnp.concatenate(parts, axis=0)
        inc = lax.dot_general(
            scaled, gain_all[:, lanes], (((1,), (1,)), ((), ())), preferred_element_type=f32
        )
        x = xt[cells, :] + inc
        xt[cells, :] = x
        if centring:
            mean = jnp.sum(x, axis=1, keepdims=True) * (1.0 / members)
            cent[cells, :] = (x - mean).astype(bf16)

    def sweep(first_q, n_q, first_slot, n_slots, side=False, centring=False):
        def step(i):
            q = first_q + i // row_groups
            update(q, i % row_groups, first_slot, n_slots, side, centring)

        repeat(n_q * row_groups, min(UNROLL, n_q * row_groups), step)

    def one_batch(k, carry):
        chosen = order_s[k]

        def gather(i, inner):
            for j in range(16):
                s = i * 16 + j
                cell = cell_s[chosen, 0, 0, s]
                chunk = (cell & (cols - 1)) >> REACH_BITS
                row = cell >> COL_BITS
                place = chunk * chunk_cells + row * REACH + (cell & (REACH - 1))
                hx[pl.ds(s, 1), :] = xt[pl.ds(place, 1), :]
            return inner

        lax.fori_loop(0, slots // 16, gather, 0)
        prior = jnp.transpose(hx[...])[:members]
        mean = jnp.sum(prior, axis=0, keepdims=True) * (1.0 / members)
        pert = prior - mean
        var = jnp.sum(pert * pert, axis=0, keepdims=True) * (1.0 / (members - 1))
        error = error_ref[chosen, 0]
        total = var + error
        shrink = 1.0 / (1.0 + jnp.sqrt(error / total))
        factor = 1.0 / ((members - 1) * total)
        live = lax.broadcasted_iota(jnp.int32, (1, slots), 1) < count_s[chosen, 0, 0]
        gain = factor * (value_ref[chosen, 0] - mean - shrink * pert)
        cell = cell_ref[chosen, 0]
        tail = jnp.concatenate(
            [
                (cell >> COL_BITS).astype(f32),
                (cell & (cols - 1)).astype(f32),
                radius_ref[chosen, 0].astype(f32),
                jnp.zeros((TAIL - 3, slots), f32),
            ],
            axis=0,
        )
        packets[k, 0, :members, :] = jnp.where(live, pert, 0.0).astype(bf16)
        packets[k, 0, members : 2 * members, :] = jnp.where(live, gain, 0.0).astype(bf16)
        packets[k, 0, 2 * members :, :] = tail.astype(bf16)
        at_sides(lambda slot: outgoing(k, slot).start())

        unpack(k, 0)
        sweep(0, chunks, 0, 1)


        @pl.when(has_north)
        def _():
            incoming(k, NORTH).wait_recv()

        @pl.when(has_south)
        def _():
            incoming(k, SOUTH).wait_recv()

        for slot in (NORTH, SOUTH):
            unpack(k, slot)
        sweep(1, chunks - 2, 1, 2, centring=True)
        sweep(0, 1, 1, 2)
        sweep(chunks - 1, 1, 1, 2)

        @pl.when(has_north)
        def _():
            for slot in (3, 6):
                incoming(k, slot).wait_recv()

        @pl.when(has_south)
        def _():
            for slot in (5, 8):
                incoming(k, slot).wait_recv()

        for slot in (WEST, EAST):
            incoming(k, slot).wait_recv()
        for slot in range(3, 9):
            unpack(k, slot)
        sweep(0, 1, 3, 3, side=True, centring=True)
        sweep(chunks - 1, 1, 6, 3, side=True, centring=True)
        at_sides(lambda slot: outgoing(k, slot).wait_send())
        return carry

    lax.fori_loop(0, batches, one_batch, 0)

    def store_row(r):
        pieces = [
            xt[pl.ds(pl.multiple_of(q * chunk_cells + r * REACH, REACH), REACH), :]
            for q in range(chunks)
        ]
        v = jnp.transpose(jnp.concatenate(pieces, axis=0))
        out_ref[pl.ds(r, members, stride=rows), :] = v[:members]

    repeat(rows, 4, store_row)


def local(ensemble, obs_value, obs_error, obs_cell, obs_radius, obs_count, batch_order):
    members, levels, rows, cols = ensemble.shape
    batches = obs_cell.shape[0]
    slots = obs_cell.shape[-1]
    assert levels == 1 and cols == LANES and slots == LANES and rows == REACH
    n_lat, n_lon = lax.axis_size("lat"), lax.axis_size("lon")
    padded = -(-members // LANES) * LANES
    cells = rows * cols
    tiles = len(OFFSETS)
    vmem = pl.BlockSpec(memory_space=pltpu.VMEM)
    smem = pl.BlockSpec(memory_space=pltpu.SMEM)
    f32, bf16 = jnp.float32, jnp.bfloat16
    out = pl.pallas_call(
        functools.partial(kernel, (members, rows, cols, slots, batches, n_lat, n_lon)),
        out_shape=jax.ShapeDtypeStruct((members * rows, cols), f32),
        in_specs=[smem, smem, smem, vmem, vmem, vmem, vmem, vmem],
        out_specs=vmem,
        scratch_shapes=[
            pltpu.VMEM((cells, padded), f32),
            pltpu.VMEM((cells, padded), bf16),
            pltpu.VMEM((slots, padded), f32),
            pltpu.VMEM((batches, tiles, 2 * members + TAIL, slots), bf16),
            pltpu.VMEM((padded, tiles * slots), bf16),
            pltpu.VMEM((padded, tiles * slots), bf16),
            pltpu.VMEM((rows, tiles * slots), f32),
            pltpu.VMEM((rows, tiles * slots), f32),
            pltpu.VMEM((cols, 3 * slots), f32),
            pltpu.VMEM((cols, 3 * slots), f32),
            pltpu.VMEM((REACH, 6 * slots), f32),
            pltpu.VMEM((REACH, 6 * slots), f32),
            pltpu.SemaphoreType.DMA((batches, tiles)),
            pltpu.SemaphoreType.DMA((batches, tiles)),
        ],
        compiler_params=pltpu.CompilerParams(
            collective_id=0, has_side_effects=True, vmem_limit_bytes=32 * 1024 * 1024
        ),
    )(
        batch_order,
        obs_count,
        obs_cell,
        ensemble.reshape(members * rows, cols),
        obs_value,
        obs_error,
        obs_cell,
        obs_radius,
    )
    return out.reshape(ensemble.shape)


def solution(mesh):
    return jax.shard_map(
        local,
        mesh=mesh,
        in_specs=(
            P(None, None, "lat", "lon"),
            P(None, "lat", "lon", None),
            P(None, "lat", "lon", None),
            P(None, "lat", "lon", None),
            P(None, "lat", "lon", None),
            P(None, "lat", "lon"),
            P(),
        ),
        out_specs=P(None, None, "lat", "lon"),
        check_vma=False,
    )
```

```python
import functools

import jax
import jax.numpy as jnp
from jax import lax
from jax.experimental import pallas as pl
from jax.experimental.pallas import tpu as pltpu
from jax.sharding import PartitionSpec as P

REACH = 32
LANES = 128
COL_BITS = 7
REACH_BITS = 5
TAIL = 16
UNROLL = 8
GROUP = 8

OFFSETS = ((0, 0), (-1, 0), (1, 0), (-1, -1), (0, -1), (1, -1), (-1, 1), (0, 1), (1, 1))
NORTH, SOUTH, WEST, EAST = 1, 2, 4, 7
PASSED_NORTH = ((WEST, 5), (EAST, 8))
PASSED_SOUTH = ((WEST, 3), (EAST, 6))


def repeat(count, unroll, body):
    def step(i, carry):
        for j in range(unroll):
            body(i * unroll + j)
        return carry

    lax.fori_loop(0, count // unroll, step, 0)


def opposite(slot):
    dy, dx = OFFSETS[slot]
    return OFFSETS.index((-dy, -dx))


def kernel(
    dims,
    order_s,
    count_s,
    cell_s,
    x_ref,
    value_ref,
    error_ref,
    cell_ref,
    radius_ref,
    out_ref,
    xt,
    cent,
    hx,
    packets,
    hp_all,
    gain_all,
    reach_lat,
    decay_lat,
    gap_mid,
    decay_mid,
    gap_side,
    decay_side,
    send_sem,
    recv_sem,
):
    members, rows, cols, slots, batches, n_lat, n_lon = dims
    padded = xt.shape[1]
    chunks = cols // REACH
    chunk_cells = rows * REACH
    row_groups = rows // GROUP
    block = GROUP * REACH
    f32, bf16 = jnp.float32, jnp.bfloat16
    lat = lax.axis_index("lat")
    lon = lax.axis_index("lon")
    has_north = lat > 0
    has_south = lat < n_lat - 1

    def device(slot):
        dy, dx = OFFSETS[slot]
        return (lat + dy, lax.rem(lon + dx + n_lon, n_lon))

    def at_sides(action):
        for slot in (WEST, EAST):
            action(slot)

        @pl.when(has_north)
        def _():
            action(NORTH)

        @pl.when(has_south)
        def _():
            action(SOUTH)

    packets[...] = jnp.zeros_like(packets)
    barrier = pltpu.get_barrier_semaphore()

    def greet(slot):
        pl.semaphore_signal(
            barrier, inc=1, device_id=device(slot), device_id_type=pl.DeviceIdType.MESH
        )

    at_sides(greet)

    hp_all[...] = jnp.zeros_like(hp_all)
    gain_all[...] = jnp.zeros_like(gain_all)

    def centre(start, size):
        x = xt[pl.ds(start, size), :]
        mean = jnp.sum(x, axis=1, keepdims=True) * (1.0 / members)
        cent[pl.ds(start, size), :] = (x - mean).astype(bf16)

    def load_row(r):
        v = x_ref[pl.ds(r, members, stride=rows), :]
        v = jnp.concatenate([v, jnp.zeros((padded - members, cols), f32)], axis=0)
        vt = jnp.transpose(v)
        mean = jnp.sum(vt, axis=1, keepdims=True) * (1.0 / members)
        vc = (vt - mean).astype(bf16)
        for q in range(chunks):
            start = pl.multiple_of(q * chunk_cells + r * REACH, REACH)
            xt[pl.ds(start, REACH), :] = vt[q * REACH : (q + 1) * REACH]
            cent[pl.ds(start, REACH), :] = vc[q * REACH : (q + 1) * REACH]

    repeat(rows, 4, load_row)

    above = (lat + n_lat - 1) // n_lat
    below = (2 * n_lat - 2 - lat) // n_lat
    pl.semaphore_wait(barrier, 2 + above + below)

    def moved(k, source, target, sender, toward):
        return pltpu.make_async_remote_copy(
            src_ref=packets.at[k, source],
            dst_ref=packets.at[k, target],
            send_sem=send_sem.at[k, sender],
            recv_sem=recv_sem.at[k, target],
            device_id=device(toward),
            device_id_type=pl.DeviceIdType.MESH,
        )

    def outgoing(k, slot):
        return moved(k, 0, opposite(slot), slot, slot)

    def incoming(k, slot):
        return moved(k, 0, slot, slot, EAST)

    def pass_on(k, action):
        for passed, toward, present in (
            (PASSED_NORTH, NORTH, has_north),
            (PASSED_SOUTH, SOUTH, has_south),
        ):

            @pl.when(present)
            def _():
                for source, target in passed:
                    action(moved(k, source, target, target, toward))

    def unpack(k, slot):
        dy, dx = OFFSETS[slot]
        lanes = slice(slot * slots, (slot + 1) * slots)
        packet = packets[k, slot]
        hp = packet[:members]
        tail = packet[2 * members :].astype(f32)
        radius = tail[2:3]
        hp_all[:members, lanes] = hp
        gain_all[:members, lanes] = packet[members : 2 * members]
        reach2 = radius * radius
        rate = -2.0 / jnp.maximum(reach2, 1.0)
        row_ids = lax.broadcasted_iota(jnp.int32, (rows, slots), 0).astype(f32)
        dlat = row_ids - (tail[0:1] + float(dy * rows))
        dlat2 = dlat * dlat
        reach_lat[:, lanes] = reach2 - dlat2
        decay_lat[:, lanes] = jnp.exp(dlat2 * rate)
        if dx == 0:
            col_ids = lax.broadcasted_iota(jnp.int32, (cols, slots), 0).astype(f32)
            dlon = col_ids - tail[1:2]
            gap_ref, decay_ref, here = gap_mid, decay_mid, lanes
        else:
            first = 0 if dx < 0 else cols - REACH
            col_ids = lax.broadcasted_iota(jnp.int32, (REACH, slots), 0).astype(f32)
            dlon = col_ids + float(first - dx * cols) - tail[1:2]
            gap_ref, decay_ref = gap_side, decay_side
            here = slice((slot - 3) * slots, (slot - 2) * slots)
        dlon2 = dlon * dlon
        gap_ref[:, here] = dlon2
        decay_ref[:, here] = jnp.exp(dlon2 * rate)

    def update(q, group, first_slot, n_slots, side, centring):
        lanes = slice(first_slot * slots, (first_slot + n_slots) * slots)
        width = n_slots * slots
        cells = pl.ds(pl.multiple_of(q * chunk_cells + group * block, block), block)
        cov = jnp.dot(cent[cells, :], hp_all[:, lanes], preferred_element_type=f32)
        if side:
            here = slice((first_slot - 3) * slots, (first_slot - 3 + n_slots) * slots)
            gap, decay = gap_side[:, here], decay_side[:, here]
        else:
            columns = pl.ds(pl.multiple_of(q * REACH, REACH), REACH)
            gap, decay = gap_mid[columns, lanes], decay_mid[columns, lanes]
        lat_rows = pl.ds(pl.multiple_of(group * GROUP, GROUP), GROUP)
        reach = reach_lat[lat_rows, lanes]
        fade = decay_lat[lat_rows, lanes]
        parts = []
        for r in range(GROUP):
            weight = jnp.where(gap <= reach[r : r + 1], decay * fade[r : r + 1], 0.0)
            parts.append((cov[r * REACH : (r + 1) * REACH] * weight).astype(bf16))
        scaled = jnp.concatenate(parts, axis=0)
        inc = lax.dot_general(
            scaled, gain_all[:, lanes], (((1,), (1,)), ((), ())), preferred_element_type=f32
        )
        x = xt[cells, :] + inc
        xt[cells, :] = x
        if centring:
            mean = jnp.sum(x, axis=1, keepdims=True) * (1.0 / members)
            cent[cells, :] = (x - mean).astype(bf16)

    def sweep(first_q, n_q, first_slot, n_slots, side=False, centring=False):
        def step(i):
            q = first_q + i // row_groups
            update(q, i % row_groups, first_slot, n_slots, side, centring)

        repeat(n_q * row_groups, min(UNROLL, n_q * row_groups), step)

    def one_batch(k, carry):
        chosen = order_s[k]

        def gather(i, inner):
            for j in range(16):
                s = i * 16 + j
                cell = cell_s[chosen, 0, 0, s]
                chunk = (cell & (cols - 1)) >> REACH_BITS
                row = cell >> COL_BITS
                place = chunk * chunk_cells + row * REACH + (cell & (REACH - 1))
                hx[pl.ds(s, 1), :] = xt[pl.ds(place, 1), :]
            return inner

        lax.fori_loop(0, slots // 16, gather, 0)
        prior = jnp.transpose(hx[...])[:members]
        mean = jnp.sum(prior, axis=0, keepdims=True) * (1.0 / members)
        pert = prior - mean
        var = jnp.sum(pert * pert, axis=0, keepdims=True) * (1.0 / (members - 1))
        error = error_ref[chosen, 0]
        total = var + error
        shrink = 1.0 / (1.0 + jnp.sqrt(error / total))
        factor = 1.0 / ((members - 1) * total)
        live = lax.broadcasted_iota(jnp.int32, (1, slots), 1) < count_s[chosen, 0, 0]
        gain = factor * (value_ref[chosen, 0] - mean - shrink * pert)
        cell = cell_ref[chosen, 0]
        tail = jnp.concatenate(
            [
                (cell >> COL_BITS).astype(f32),
                (cell & (cols - 1)).astype(f32),
                radius_ref[chosen, 0].astype(f32),
                jnp.zeros((TAIL - 3, slots), f32),
            ],
            axis=0,
        )
        packets[k, 0, :members, :] = jnp.where(live, pert, 0.0).astype(bf16)
        packets[k, 0, members : 2 * members, :] = jnp.where(live, gain, 0.0).astype(bf16)
        packets[k, 0, 2 * members :, :] = tail.astype(bf16)
        at_sides(lambda slot: outgoing(k, slot).start())

        unpack(k, 0)
        sweep(0, chunks, 0, 1)

        for slot in (WEST, EAST):
            incoming(k, slot).wait_recv()
        pass_on(k, lambda copy: copy.start())

        @pl.when(has_north)
        def _():
            incoming(k, NORTH).wait_recv()

        @pl.when(has_south)
        def _():
            incoming(k, SOUTH).wait_recv()

        for slot in (NORTH, SOUTH, WEST, EAST):
            unpack(k, slot)
        sweep(1, chunks - 2, 1, 2, centring=True)
        sweep(0, 1, 1, 2)
        sweep(chunks - 1, 1, 1, 2)

        @pl.when(has_north)
        def _():
            for _, slot in PASSED_SOUTH:
                incoming(k, slot).wait_recv()

        @pl.when(has_south)
        def _():
            for _, slot in PASSED_NORTH:
                incoming(k, slot).wait_recv()

        for _, slot in PASSED_NORTH + PASSED_SOUTH:
            unpack(k, slot)
        sweep(0, 1, 3, 3, side=True, centring=True)
        sweep(chunks - 1, 1, 6, 3, side=True, centring=True)
        at_sides(lambda slot: outgoing(k, slot).wait_send())
        pass_on(k, lambda copy: copy.wait_send())
        return carry

    lax.fori_loop(0, batches, one_batch, 0)

    def store_row(r):
        pieces = [
            xt[pl.ds(pl.multiple_of(q * chunk_cells + r * REACH, REACH), REACH), :]
            for q in range(chunks)
        ]
        v = jnp.transpose(jnp.concatenate(pieces, axis=0))
        out_ref[pl.ds(r, members, stride=rows), :] = v[:members]

    repeat(rows, 4, store_row)


def local(ensemble, obs_value, obs_error, obs_cell, obs_radius, obs_count, batch_order):
    members, levels, rows, cols = ensemble.shape
    batches = obs_cell.shape[0]
    slots = obs_cell.shape[-1]
    assert levels == 1 and cols == LANES and slots == LANES and rows == REACH
    n_lat, n_lon = lax.axis_size("lat"), lax.axis_size("lon")
    padded = -(-members // LANES) * LANES
    cells = rows * cols
    tiles = len(OFFSETS)
    vmem = pl.BlockSpec(memory_space=pltpu.VMEM)
    smem = pl.BlockSpec(memory_space=pltpu.SMEM)
    f32, bf16 = jnp.float32, jnp.bfloat16
    out = pl.pallas_call(
        functools.partial(kernel, (members, rows, cols, slots, batches, n_lat, n_lon)),
        out_shape=jax.ShapeDtypeStruct((members * rows, cols), f32),
        in_specs=[smem, smem, smem, vmem, vmem, vmem, vmem, vmem],
        out_specs=vmem,
        scratch_shapes=[
            pltpu.VMEM((cells, padded), f32),
            pltpu.VMEM((cells, padded), bf16),
            pltpu.VMEM((slots, padded), f32),
            pltpu.VMEM((batches, tiles, 2 * members + TAIL, slots), bf16),
            pltpu.VMEM((padded, tiles * slots), bf16),
            pltpu.VMEM((padded, tiles * slots), bf16),
            pltpu.VMEM((rows, tiles * slots), f32),
            pltpu.VMEM((rows, tiles * slots), f32),
            pltpu.VMEM((cols, 3 * slots), f32),
            pltpu.VMEM((cols, 3 * slots), f32),
            pltpu.VMEM((REACH, 6 * slots), f32),
            pltpu.VMEM((REACH, 6 * slots), f32),
            pltpu.SemaphoreType.DMA((batches, tiles)),
            pltpu.SemaphoreType.DMA((batches, tiles)),
        ],
        compiler_params=pltpu.CompilerParams(
            collective_id=0, has_side_effects=True, vmem_limit_bytes=32 * 1024 * 1024
        ),
    )(
        batch_order,
        obs_count,
        obs_cell,
        ensemble.reshape(members * rows, cols),
        obs_value,
        obs_error,
        obs_cell,
        obs_radius,
    )
    return out.reshape(ensemble.shape)


def solution(mesh):
    return jax.shard_map(
        local,
        mesh=mesh,
        in_specs=(
            P(None, None, "lat", "lon"),
            P(None, "lat", "lon", None),
            P(None, "lat", "lon", None),
            P(None, "lat", "lon", None),
            P(None, "lat", "lon", None),
            P(None, "lat", "lon"),
            P(),
        ),
        out_specs=P(None, None, "lat", "lon"),
        check_vma=False,
    )
```

```python
import functools

import jax
import jax.numpy as jnp
from jax import lax
from jax.experimental import pallas as pl
from jax.experimental.pallas import tpu as pltpu
from jax.sharding import PartitionSpec as P

REACH = 32
LANES = 128
COL_BITS = 7
REACH_BITS = 5
TAIL = 16
UNROLL = 8
GROUP = 8

OFFSETS = ((0, 0), (-1, 0), (1, 0), (-1, -1), (0, -1), (1, -1), (-1, 1), (0, 1), (1, 1))
NORTH, SOUTH, WEST, EAST = 1, 2, 4, 7
PASSED_NORTH = ((WEST, 5), (EAST, 8))
PASSED_SOUTH = ((WEST, 3), (EAST, 6))


def repeat(count, unroll, body):
    def step(i, carry):
        for j in range(unroll):
            body(i * unroll + j)
        return carry

    lax.fori_loop(0, count // unroll, step, 0)


def opposite(slot):
    dy, dx = OFFSETS[slot]
    return OFFSETS.index((-dy, -dx))


def kernel(
    dims,
    order_s,
    count_s,
    cell_s,
    x_ref,
    value_ref,
    error_ref,
    cell_ref,
    radius_ref,
    out_ref,
    xt,
    cent,
    hx,
    packets,
    hp_all,
    gain_all,
    reach_lat,
    decay_lat,
    gap_mid,
    decay_mid,
    gap_side,
    decay_side,
    send_sem,
    recv_sem,
):
    members, rows, cols, slots, batches, n_lat, n_lon = dims
    padded = xt.shape[1]
    chunks = cols // REACH
    chunk_cells = rows * REACH
    row_groups = rows // GROUP
    block = GROUP * REACH
    f32, bf16 = jnp.float32, jnp.bfloat16
    lat = lax.axis_index("lat")
    lon = lax.axis_index("lon")
    has_north = lat > 0
    has_south = lat < n_lat - 1

    def device(slot):
        dy, dx = OFFSETS[slot]
        return (lat + dy, lax.rem(lon + dx + n_lon, n_lon))

    def at_sides(action):
        for slot in (WEST, EAST):
            action(slot)

        @pl.when(has_north)
        def _():
            action(NORTH)

        @pl.when(has_south)
        def _():
            action(SOUTH)

    packets[...] = jnp.zeros_like(packets)
    barrier = pltpu.get_barrier_semaphore()

    def greet(slot):
        pl.semaphore_signal(
            barrier, inc=1, device_id=device(slot), device_id_type=pl.DeviceIdType.MESH
        )

    at_sides(greet)

    hp_all[...] = jnp.zeros_like(hp_all)
    gain_all[...] = jnp.zeros_like(gain_all)

    def centre(start, size):
        x = xt[pl.ds(start, size), :]
        mean = jnp.sum(x, axis=1, keepdims=True) * (1.0 / members)
        cent[pl.ds(start, size), :] = (x - mean).astype(bf16)

    def load_row(r):
        v = x_ref[pl.ds(r, members, stride=rows), :]
        v = jnp.concatenate([v, jnp.zeros((padded - members, cols), f32)], axis=0)
        vt = jnp.transpose(v)
        mean = jnp.sum(vt, axis=1, keepdims=True) * (1.0 / members)
        vc = (vt - mean).astype(bf16)
        for q in range(chunks):
            start = pl.multiple_of(q * chunk_cells + r * REACH, REACH)
            xt[pl.ds(start, REACH), :] = vt[q * REACH : (q + 1) * REACH]
            cent[pl.ds(start, REACH), :] = vc[q * REACH : (q + 1) * REACH]

    repeat(rows, 8, load_row)

    above = (lat + n_lat - 1) // n_lat
    below = (2 * n_lat - 2 - lat) // n_lat
    pl.semaphore_wait(barrier, 2 + above + below)

    def moved(k, source, target, sender, toward):
        return pltpu.make_async_remote_copy(
            src_ref=packets.at[k, source],
            dst_ref=packets.at[k, target],
            send_sem=send_sem.at[k, sender],
            recv_sem=recv_sem.at[k, target],
            device_id=device(toward),
            device_id_type=pl.DeviceIdType.MESH,
        )

    def outgoing(k, slot):
        return moved(k, 0, opposite(slot), slot, slot)

    def incoming(k, slot):
        return moved(k, 0, slot, slot, EAST)

    def pass_on(k, action):
        for passed, toward, present in (
            (PASSED_NORTH, NORTH, has_north),
            (PASSED_SOUTH, SOUTH, has_south),
        ):

            @pl.when(present)
            def _():
                for source, target in passed:
                    action(moved(k, source, target, target, toward))

    def unpack(k, slot):
        dy, dx = OFFSETS[slot]
        lanes = slice(slot * slots, (slot + 1) * slots)
        packet = packets[k, slot]
        hp = packet[:members]
        tail = packet[2 * members :].astype(f32)
        radius = tail[2:3]
        hp_all[:members, lanes] = hp
        gain_all[:members, lanes] = packet[members : 2 * members]
        reach2 = radius * radius
        rate = -2.0 / jnp.maximum(reach2, 1.0)
        row_ids = lax.broadcasted_iota(jnp.int32, (rows, slots), 0).astype(f32)
        dlat = row_ids - (tail[0:1] + float(dy * rows))
        dlat2 = dlat * dlat
        reach_lat[:, lanes] = reach2 - dlat2
        decay_lat[:, lanes] = jnp.exp(dlat2 * rate)
        if dx == 0:
            col_ids = lax.broadcasted_iota(jnp.int32, (cols, slots), 0).astype(f32)
            dlon = col_ids - tail[1:2]
            gap_ref, decay_ref, here = gap_mid, decay_mid, lanes
        else:
            first = 0 if dx < 0 else cols - REACH
            col_ids = lax.broadcasted_iota(jnp.int32, (REACH, slots), 0).astype(f32)
            dlon = col_ids + float(first - dx * cols) - tail[1:2]
            gap_ref, decay_ref = gap_side, decay_side
            here = slice((slot - 3) * slots, (slot - 2) * slots)
        dlon2 = dlon * dlon
        gap_ref[:, here] = dlon2
        decay_ref[:, here] = jnp.exp(dlon2 * rate)

    def update(q, group, first_slot, n_slots, side, centring):
        lanes = slice(first_slot * slots, (first_slot + n_slots) * slots)
        width = n_slots * slots
        cells = pl.ds(pl.multiple_of(q * chunk_cells + group * block, block), block)
        cov = jnp.dot(cent[cells, :], hp_all[:, lanes], preferred_element_type=f32)
        if side:
            here = slice((first_slot - 3) * slots, (first_slot - 3 + n_slots) * slots)
            gap, decay = gap_side[:, here], decay_side[:, here]
        else:
            columns = pl.ds(pl.multiple_of(q * REACH, REACH), REACH)
            gap, decay = gap_mid[columns, lanes], decay_mid[columns, lanes]
        lat_rows = pl.ds(pl.multiple_of(group * GROUP, GROUP), GROUP)
        reach = reach_lat[lat_rows, lanes]
        fade = decay_lat[lat_rows, lanes]
        parts = []
        for r in range(GROUP):
            weight = jnp.where(gap <= reach[r : r + 1], decay * fade[r : r + 1], 0.0)
            parts.append((cov[r * REACH : (r + 1) * REACH] * weight).astype(bf16))
        scaled = jnp.concatenate(parts, axis=0)
        inc = lax.dot_general(
            scaled, gain_all[:, lanes], (((1,), (1,)), ((), ())), preferred_element_type=f32
        )
        x = xt[cells, :] + inc
        xt[cells, :] = x
        if centring:
            mean = jnp.sum(x, axis=1, keepdims=True) * (1.0 / members)
            cent[cells, :] = (x - mean).astype(bf16)

    def sweep(first_q, n_q, first_slot, n_slots, side=False, centring=False):
        def step(i):
            q = first_q + i // row_groups
            update(q, i % row_groups, first_slot, n_slots, side, centring)

        repeat(n_q * row_groups, min(UNROLL, n_q * row_groups), step)

    def one_batch(k, carry):
        chosen = order_s[k]

        def gather(i, inner):
            for j in range(16):
                s = i * 16 + j
                cell = cell_s[chosen, 0, 0, s]
                chunk = (cell & (cols - 1)) >> REACH_BITS
                row = cell >> COL_BITS
                place = chunk * chunk_cells + row * REACH + (cell & (REACH - 1))
                hx[pl.ds(s, 1), :] = xt[pl.ds(place, 1), :]
            return inner

        lax.fori_loop(0, slots // 16, gather, 0)
        prior = jnp.transpose(hx[...])[:members]
        mean = jnp.sum(prior, axis=0, keepdims=True) * (1.0 / members)
        pert = prior - mean
        var = jnp.sum(pert * pert, axis=0, keepdims=True) * (1.0 / (members - 1))
        error = error_ref[chosen, 0]
        total = var + error
        shrink = 1.0 / (1.0 + jnp.sqrt(error / total))
        factor = 1.0 / ((members - 1) * total)
        live = lax.broadcasted_iota(jnp.int32, (1, slots), 1) < count_s[chosen, 0, 0]
        gain = factor * (value_ref[chosen, 0] - mean - shrink * pert)
        cell = cell_ref[chosen, 0]
        tail = jnp.concatenate(
            [
                (cell >> COL_BITS).astype(f32),
                (cell & (cols - 1)).astype(f32),
                radius_ref[chosen, 0].astype(f32),
                jnp.zeros((TAIL - 3, slots), f32),
            ],
            axis=0,
        )
        packets[k, 0, :members, :] = jnp.where(live, pert, 0.0).astype(bf16)
        packets[k, 0, members : 2 * members, :] = jnp.where(live, gain, 0.0).astype(bf16)
        packets[k, 0, 2 * members :, :] = tail.astype(bf16)
        at_sides(lambda slot: outgoing(k, slot).start())

        unpack(k, 0)
        sweep(0, chunks, 0, 1)

        for slot in (WEST, EAST):
            incoming(k, slot).wait_recv()
        pass_on(k, lambda copy: copy.start())

        @pl.when(has_north)
        def _():
            incoming(k, NORTH).wait_recv()

        @pl.when(has_south)
        def _():
            incoming(k, SOUTH).wait_recv()

        for slot in (NORTH, SOUTH, WEST, EAST):
            unpack(k, slot)
        sweep(1, chunks - 2, 1, 2, centring=True)
        sweep(0, 1, 1, 2)
        sweep(chunks - 1, 1, 1, 2)

        @pl.when(has_north)
        def _():
            for _, slot in PASSED_SOUTH:
                incoming(k, slot).wait_recv()

        @pl.when(has_south)
        def _():
            for _, slot in PASSED_NORTH:
                incoming(k, slot).wait_recv()

        for _, slot in PASSED_NORTH + PASSED_SOUTH:
            unpack(k, slot)
        sweep(0, 1, 3, 3, side=True, centring=True)
        sweep(chunks - 1, 1, 6, 3, side=True, centring=True)
        at_sides(lambda slot: outgoing(k, slot).wait_send())
        pass_on(k, lambda copy: copy.wait_send())
        return carry

    lax.fori_loop(0, batches, one_batch, 0)

    def store_row(r):
        pieces = [
            xt[pl.ds(pl.multiple_of(q * chunk_cells + r * REACH, REACH), REACH), :]
            for q in range(chunks)
        ]
        v = jnp.transpose(jnp.concatenate(pieces, axis=0))
        out_ref[pl.ds(r, members, stride=rows), :] = v[:members]

    repeat(rows, 8, store_row)


def local(ensemble, obs_value, obs_error, obs_cell, obs_radius, obs_count, batch_order):
    members, levels, rows, cols = ensemble.shape
    batches = obs_cell.shape[0]
    slots = obs_cell.shape[-1]
    assert levels == 1 and cols == LANES and slots == LANES and rows == REACH
    n_lat, n_lon = lax.axis_size("lat"), lax.axis_size("lon")
    padded = -(-members // LANES) * LANES
    cells = rows * cols
    tiles = len(OFFSETS)
    vmem = pl.BlockSpec(memory_space=pltpu.VMEM)
    smem = pl.BlockSpec(memory_space=pltpu.SMEM)
    f32, bf16 = jnp.float32, jnp.bfloat16
    out = pl.pallas_call(
        functools.partial(kernel, (members, rows, cols, slots, batches, n_lat, n_lon)),
        out_shape=jax.ShapeDtypeStruct((members * rows, cols), f32),
        in_specs=[smem, smem, smem, vmem, vmem, vmem, vmem, vmem],
        out_specs=vmem,
        scratch_shapes=[
            pltpu.VMEM((cells, padded), f32),
            pltpu.VMEM((cells, padded), bf16),
            pltpu.VMEM((slots, padded), f32),
            pltpu.VMEM((batches, tiles, 2 * members + TAIL, slots), bf16),
            pltpu.VMEM((padded, tiles * slots), bf16),
            pltpu.VMEM((padded, tiles * slots), bf16),
            pltpu.VMEM((rows, tiles * slots), f32),
            pltpu.VMEM((rows, tiles * slots), f32),
            pltpu.VMEM((cols, 3 * slots), f32),
            pltpu.VMEM((cols, 3 * slots), f32),
            pltpu.VMEM((REACH, 6 * slots), f32),
            pltpu.VMEM((REACH, 6 * slots), f32),
            pltpu.SemaphoreType.DMA((batches, tiles)),
            pltpu.SemaphoreType.DMA((batches, tiles)),
        ],
        compiler_params=pltpu.CompilerParams(
            collective_id=0, has_side_effects=True, vmem_limit_bytes=32 * 1024 * 1024
        ),
    )(
        batch_order,
        obs_count,
        obs_cell,
        ensemble.reshape(members * rows, cols),
        obs_value,
        obs_error,
        obs_cell,
        obs_radius,
    )
    return out.reshape(ensemble.shape)


def solution(mesh):
    return jax.shard_map(
        local,
        mesh=mesh,
        in_specs=(
            P(None, None, "lat", "lon"),
            P(None, "lat", "lon", None),
            P(None, "lat", "lon", None),
            P(None, "lat", "lon", None),
            P(None, "lat", "lon", None),
            P(None, "lat", "lon"),
            P(),
        ),
        out_specs=P(None, None, "lat", "lon"),
        check_vma=False,
    )
```
